256 devices in a mesh: seq: 128 (over y, z, x), head: 2 (over core).
Axes of the slice: x: 4, y: 4, z: 8, core: 2. Of those that a mesh axis runs over, the one named last changes fastest.
Arguments:
- tokens: bfloat16 [1024, 64, 2048], P('seq'), may hold values from -64 to 64
- w_qkv: bfloat16 [3, 2048, 1024], P(None, None, 'head'), may hold values from -1 to 1
- conv_taps: float32 [3, 3, 1024], P(None, None, 'head'), may hold values from -1 to 1
- w_out: bfloat16 [1024, 2048], P('head'), may hold values from -0.1875 to 0.1875
- episode_start: int32 [1024], P('seq'), may hold values from 0 to 1023, as said below
Outputs:
- sublayer_out: bfloat16 [1024, 64, 2048], P('seq', None, 'head')
The draws below stay inside these ranges and needn't reach their ends.
Inputs may be any that keep to these rules, and one draw needn't show every extreme that they name: episode_start[t] is the first frame of the episode holding frame t; episodes are runs of 1 to 64 consecutive frames, and one has exactly 64.
All inputs are finite; a program needn't handle non-finite values.
Results may differ from the reference program's by a relative error of at most 0.006.
The reference program's roundings to bfloat16 on the way (of `normed`, `convolved`, `probs` and `attended`) count: a program that leaves them out, or rounds other values in their place, can miss the bound.
Values may be sent and summed in bfloat16 or wider, within the bound.
No kernel may reach another device: no remote copies, remote signals or barrier semaphores. Data moves between devices by JAX's collectives and lax.ppermute only.
A program may use at most 128 MiB of HBM per device.

```python
import math
import jax
import jax.numpy as jnp
from jax import lax

D = 2048
HEAD_DIM = 128
HEADS = 8
POSITIONS = 64
FRAMES_DEV = 8
REACH = 8
FRAMES = 1024
EPISODE_MAX = 64


def draw_tokens(key, part):
    key_base, key_rows, key_cols = jax.random.split(jax.random.fold_in(key, 11), 3)
    row_scale = jnp.exp(jax.random.uniform(key_rows, (FRAMES, POSITIONS, 1), jnp.float32, 0.0, math.log(10.0)))
    col_scale = jnp.exp(jax.random.uniform(key_cols, (1, 1, D), jnp.float32, 0.0, math.log(10.0)))
    base_draw = jax.random.normal(key_base, (FRAMES, POSITIONS, D), jnp.float32)
    return jnp.clip(base_draw * row_scale * col_scale / 10.0, -64.0, 64.0).astype(jnp.bfloat16)


def draw_w_qkv(key, part):
    key_base = jax.random.fold_in(jax.random.fold_in(key, 23), 0)
    weights = jax.random.normal(key_base, (3, D, HEADS * HEAD_DIM), jnp.float32) / math.sqrt(D)
    return jnp.clip(weights, -1.0, 1.0).astype(jnp.bfloat16)


def draw_episode_start(key, part):
    key_off, key_busy, key_cut, key_full = jax.random.split(jax.random.fold_in(key, 37), 4)
    frame_ids = jnp.arange(FRAMES, dtype=jnp.int32)
    offset = jax.random.randint(key_off, (), 0, EPISODE_MAX)
    shifted_ids = frame_ids - offset
    window_ids = jnp.floor_divide(shifted_ids, EPISODE_MAX)
    forced = jnp.remainder(shifted_ids, EPISODE_MAX) == 0
    busy_flags = jax.random.randint(key_busy, (FRAMES // EPISODE_MAX + 2,), 0, 2)
    full_window = jax.random.randint(key_full, (), 0, FRAMES // EPISODE_MAX - 1)
    busy_flags = busy_flags.at[full_window + 1].set(0)
    busy_here = busy_flags[window_ids + 1]
    extra_cuts = jax.random.randint(key_cut, (FRAMES,), 0, 6) == 0
    boundary = forced | extra_cuts & (busy_here == 1) | (frame_ids == 0)
    return lax.cummax(jnp.where(boundary, frame_ids, 0), axis=0).astype(jnp.int32)


def steps_of(own_key, dims, pieces, low, largest):
    factor_of, own = 1.0, jax.random.fold_in(own_key, 6)
    for position, shards_of in pieces:
        draws = jnp.exp(jax.random.uniform(jax.random.fold_in(own, position), (shards_of,), jnp.float32, low / len(pieces), largest / len(pieces)))
        factor_of = factor_of * jnp.repeat(draws, dims[position] // shards_of).reshape([-1 if axis == position else 1 for axis in range(len(dims))])
    return factor_of


def scatter_about(stream_key, extent, scale, bound, cuts=(), kind=jnp.bfloat16):
    gain = steps_of(stream_key, extent, cuts, -0.22, 0.18) if cuts else 1.0
    values = jax.random.normal(stream_key, extent, jnp.float32) * scale * gain
    return jnp.minimum(jnp.maximum(values, -bound), bound).astype(kind)


def setup_inputs(seed: int = 0) -> dict:
    key_list = jax.random.split(jax.random.key(seed), 6)
    tokens = draw_tokens(jax.random.fold_in(key_list[5], 71), 0)
    w_qkv = draw_w_qkv(jax.random.fold_in(key_list[5], 71), 0)
    conv_taps = jnp.clip(jax.random.uniform(key_list[2], (3, 3, HEADS * HEAD_DIM), jnp.float32, -1.0, 1.0) * steps_of(key_list[2], (3, 3, HEADS * HEAD_DIM), ((2, 2),), -0.4, 0.0), -1.0, 1.0)
    w_out = scatter_about(key_list[3], (HEADS * HEAD_DIM, D), (HEADS * HEAD_DIM) ** -0.5, 0.1875, ((0, 2),))
    episode_start = draw_episode_start(jax.random.fold_in(key_list[5], 71), 0)
    return dict(tokens=tokens, w_qkv=w_qkv, conv_taps=conv_taps, w_out=w_out, episode_start=episode_start)


def attend(queries, keys_in, values_in, starts, first_query, first_key, head_dim):
    query_len, positions, inner_width = queries.shape
    key_len = keys_in.shape[0]
    head_count = inner_width // head_dim
    query_heads = queries.reshape(query_len, positions, head_count, head_dim).astype(jnp.float32)
    key_heads = keys_in.reshape(key_len, positions, head_count, head_dim).astype(jnp.float32)
    value_heads = values_in.reshape(key_len, positions, head_count, head_dim).astype(jnp.float32)
    scores = jnp.einsum('qphd,kphd->phqk', query_heads, key_heads) / math.sqrt(head_dim)
    qframe = first_query + jnp.arange(query_len, dtype=jnp.int32)
    kframe = first_key + jnp.arange(key_len, dtype=jnp.int32)
    allowed = (kframe[None, :] >= starts[:, None]) & (kframe[None, :] <= qframe[:, None])
    masked = jnp.where(allowed[None, None], scores, -1e+30)
    row_max = lax.optimization_barrier(jnp.max(masked, axis=-1, keepdims=True))
    unnorm = jnp.where(allowed[None, None], jnp.exp(masked - row_max), 0.0)
    probs = (unnorm / lax.optimization_barrier(jnp.sum(unnorm, axis=-1, keepdims=True))).astype(jnp.bfloat16)
    result = jnp.einsum('phqk,kphd->qphd', probs.astype(jnp.float32), value_heads)
    return result.reshape(query_len, positions, inner_width).astype(jnp.bfloat16)

def reference(tokens, w_qkv, conv_taps, w_out, episode_start):
    frames, positions, model_width = tokens.shape
    inner_width = w_qkv.shape[2]
    tokens_f = tokens.astype(jnp.float32)
    inv_rms = lax.rsqrt(lax.optimization_barrier(jnp.mean(tokens_f * tokens_f, axis=-1, keepdims=True)) + 1e-06)
    normed = (tokens_f * inv_rms).astype(jnp.bfloat16)
    flat_rows = normed.reshape(frames * positions, model_width)
    projected = jnp.stack([jnp.dot(flat_rows, w_qkv[slot_id], preferred_element_type=jnp.float32) for slot_id in range(3)])
    projected = projected.reshape(3, frames, positions, inner_width)
    padded = jnp.concatenate([jnp.zeros((3, 2, positions, inner_width), projected.dtype), projected], axis=1)
    frame_ids = jnp.arange(frames, dtype=jnp.int32)
    convolved = jnp.zeros_like(projected)
    for frame_lag in range(3):
        shifted = padded[:, 2 - frame_lag:2 - frame_lag + frames]
        in_episode = (frame_ids - frame_lag >= episode_start).astype(projected.dtype)
        convolved = convolved + conv_taps[frame_lag][:, None, None, :] * shifted * in_episode[None, :, None, None]
    convolved = convolved.astype(jnp.bfloat16)
    queries, keys_all, values_all = (convolved[0], convolved[1], convolved[2])
    front_len = REACH * FRAMES_DEV
    span_len = (REACH + 1) * FRAMES_DEV
    zeros_front = jnp.zeros((front_len, positions, inner_width), convolved.dtype)
    keys_padded = jnp.concatenate([zeros_front, keys_all], axis=0)
    values_padded = jnp.concatenate([zeros_front, values_all], axis=0)

    def one_block(block_id):
        first_row = (block_id * FRAMES_DEV).astype(jnp.int32)
        block_q = lax.dynamic_slice_in_dim(queries, first_row, FRAMES_DEV, 0)
        block_k = lax.dynamic_slice_in_dim(keys_padded, first_row, span_len, 0)
        block_v = lax.dynamic_slice_in_dim(values_padded, first_row, span_len, 0)
        starts = lax.dynamic_slice_in_dim(episode_start, first_row, FRAMES_DEV, 0)
        return attend(block_q, block_k, block_v, starts, first_row, first_row - front_len, HEAD_DIM)
    attended = lax.map(one_block, jnp.arange(frames // FRAMES_DEV, dtype=jnp.int32))
    attended = attended.reshape(frames * positions, inner_width)
    result = jnp.dot(attended, w_out, preferred_element_type=jnp.float32)
    return result.reshape(frames, positions, model_width).astype(jnp.bfloat16)
```

```python
import functools
import math

import jax
import jax.numpy as jnp
from jax import lax
from jax.experimental import pallas as pl
from jax.experimental.pallas import tpu as pltpu
from jax.sharding import Mesh
from jax.sharding import PartitionSpec as P

HEAD_DIM = 128
BACK = 64
PLANES, ROWS, COLS, CORES = 4, 8, 4, 2
GROUP = ROWS * COLS
LANES = 128
QUERY_BLOCK = 128
SWAP = [(0, 1), (1, 0)]


def attention_kernel(main_own, main_other, halo_own, halo_other, lag_ref, taps_ref, out_ref, pad, conv):
    frames = main_own.shape[1]
    total = BACK + frames
    half = main_own.shape[2]
    lag = lag_ref[...].astype(jnp.float32)
    pad[0:8] = jnp.zeros((8, half), jnp.float32)
    for side, (main, halo) in enumerate(((main_own, halo_own), (main_other, halo_other))):
        for kind in range(3):
            pad[8 : 8 + BACK] = halo[kind]
            pad[8 + BACK : 8 + total] = main[kind]
            for column in range(0, half, LANES):
                columns = slice(column, column + LANES)
                acc = taps_ref[side, 0, kind, columns][None, :] * pad[8 : 8 + total, columns]
                for frame_lag in (1, 2):
                    term = (
                        taps_ref[side, frame_lag, kind, columns][None, :]
                        * pad[8 - frame_lag : 8 - frame_lag + total, columns]
                    )
                    acc = acc + jnp.where(lag >= frame_lag, term, 0.0)
                conv[kind, :, side * half + column : side * half + column + LANES] = acc.astype(
                    jnp.bfloat16
                )
    keys = QUERY_BLOCK + BACK
    row = lax.broadcasted_iota(jnp.int32, (QUERY_BLOCK, keys), 0)
    col = lax.broadcasted_iota(jnp.int32, (QUERY_BLOCK, keys), 1)
    age = row + BACK - col
    for block in range(frames // QUERY_BLOCK):
        first = block * QUERY_BLOCK
        query_lag = lag_ref[BACK + first : BACK + first + QUERY_BLOCK, 0:1].astype(jnp.int32)
        allowed = (age >= 0) & (age <= query_lag)
        for head in range(2 * half // HEAD_DIM):
            columns = slice(head * HEAD_DIM, (head + 1) * HEAD_DIM)
            query = conv[0, BACK + first : BACK + first + QUERY_BLOCK, columns]
            key = conv[1, first : first + keys, columns]
            value = conv[2, first : first + keys, columns]
            scores = lax.dot_general(
                query, key, (((1,), (1,)), ((), ())), preferred_element_type=jnp.float32
            ) / math.sqrt(HEAD_DIM)
            masked = jnp.where(allowed, scores, -1e30)
            unnorm = jnp.exp(masked - jnp.max(masked, axis=-1, keepdims=True))
            unnorm = jnp.where(allowed, unnorm, 0.0)
            probs = (unnorm / jnp.sum(unnorm, axis=-1, keepdims=True)).astype(jnp.bfloat16)
            result = jnp.dot(probs, value, preferred_element_type=jnp.float32)
            out_ref[first : first + QUERY_BLOCK, columns] = result.astype(jnp.bfloat16)


def attention(main_own, main_other, halo_own, halo_other, lag, taps):
    frames, half = main_own.shape[1:]
    vmem = pl.BlockSpec(memory_space=pltpu.VMEM)
    return pl.pallas_call(
        attention_kernel,
        out_shape=jax.ShapeDtypeStruct((frames, 2 * half), jnp.bfloat16),
        in_specs=[vmem] * 6,
        out_specs=vmem,
        scratch_shapes=[
            pltpu.VMEM((8 + BACK + frames, half), jnp.float32),
            pltpu.VMEM((3, BACK + frames, 2 * half), jnp.bfloat16),
        ],
    )(main_own, main_other, halo_own, halo_other, lag, taps)


def shards(tokens, w_qkv, conv_taps, w_out, episode_start):
    frames, positions, model_width = tokens.shape
    inner_width = w_qkv.shape[2]
    share = positions // CORES
    core = lax.axis_index("core")
    device_row = lax.axis_index(("y", "z", "x"))
    out_half = model_width // CORES

    w_other = lax.ppermute(w_qkv, "core", SWAP)
    taps_other = lax.ppermute(conv_taps, "core", SWAP)
    mine = lax.dynamic_slice_in_dim(w_out, core * out_half, out_half, 1)
    theirs = lax.dynamic_slice_in_dim(w_out, (1 - core) * out_half, out_half, 1)
    w_out_other = lax.ppermute(theirs, "core", SWAP)

    tokens_f = lax.dynamic_slice_in_dim(tokens, core * share, share, 1).astype(jnp.float32)
    inv_rms = lax.rsqrt(jnp.mean(tokens_f * tokens_f, axis=-1, keepdims=True) + 1e-06)
    normed = (tokens_f * inv_rms).astype(jnp.bfloat16).transpose(1, 0, 2)
    frame_ids = device_row * frames + jnp.arange(frames, dtype=jnp.int32)
    lag = (frame_ids - episode_start).astype(jnp.bfloat16)
    packed = jnp.concatenate(
        [normed, jnp.broadcast_to(lag[None, :, None], (share, frames, LANES))], axis=2
    )
    rows = lax.all_to_all(packed, ("z", "x"), 0, 0, tiled=True)
    rows = rows.reshape(GROUP * frames, model_width + LANES)
    halo = lax.ppermute(rows[-BACK:], "y", [(y, y + 1) for y in range(PLANES - 1)])

    def project(part, weight):
        return jnp.einsum(
            "nd,cde->cne", part[:, :model_width], weight, preferred_element_type=jnp.float32
        )

    attended = attention(
        project(rows, w_qkv),
        project(rows, w_other),
        project(halo, w_qkv),
        project(halo, w_other),
        jnp.concatenate([halo[:, model_width:], rows[:, model_width:]], axis=0),
        jnp.stack([conv_taps, taps_other]),
    )
    back = lax.all_to_all(
        attended.reshape(GROUP, frames, CORES * inner_width), ("z", "x"), 0, 0, tiled=True
    )
    back_other = lax.ppermute(back, "core", SWAP)

    def output(part, first, second):
        flat = part.reshape(share * frames, CORES * inner_width)
        return (
            jnp.dot(flat[:, :inner_width], first, preferred_element_type=jnp.float32)
            + jnp.dot(flat[:, inner_width:], second, preferred_element_type=jnp.float32)
        ).astype(jnp.bfloat16).reshape(share, frames, out_half).transpose(1, 0, 2)

    out_mine = output(back, mine, w_out_other)
    out_other = output(back_other, w_out_other, mine)
    result = jnp.zeros((frames, positions, out_half), jnp.bfloat16)
    result = lax.dynamic_update_slice_in_dim(result, out_mine, core * share, 1)
    return lax.dynamic_update_slice_in_dim(result, out_other, (1 - core) * share, 1)


def solution(mesh):
    grid = Mesh(mesh.devices.reshape(PLANES, ROWS, COLS, CORES), ("y", "z", "x", "core"))
    seq = ("y", "z", "x")
    in_specs = (
        P(seq, None, None),
        P(None, None, "core"),
        P(None, None, "core"),
        P("core", None),
        P(seq),
    )
    return jax.shard_map(
        shards, mesh=grid, in_specs=in_specs, out_specs=P(seq, None, "core"), check_vma=False
    )
```

```python
import functools
import math

import jax
import jax.numpy as jnp
from jax import lax
from jax.experimental import pallas as pl
from jax.experimental.pallas import tpu as pltpu
from jax.sharding import Mesh
from jax.sharding import PartitionSpec as P

HEAD_DIM = 128
BACK = 64
PLANES, ROWS, COLS, CORES = 4, 8, 4, 2
GROUP = ROWS * COLS
LANES = 128
PAIR = 256
LIMIT = 12 * 1024 * 1024
SWAP = [(0, 1), (1, 0)]


def convolve(pad, conv, taps_ref, masks, kind, first_column, rows):
    for column in range(0, PAIR, LANES):
        columns = slice(column, column + LANES)
        taps = slice(first_column + column, first_column + column + LANES)
        acc = taps_ref[0, kind, taps][None, :] * pad[8 : 8 + rows, columns]
        for lag in (1, 2):
            acc = acc + (
                taps_ref[lag, kind, taps][None, :] * pad[8 - lag : 8 - lag + rows, columns]
            ) * masks[lag - 1]
        conv[kind, :, columns] = acc.astype(jnp.bfloat16)


def attend(query, key, value, bias):
    scores = lax.dot_general(
        query, key, (((1,), (1,)), ((), ())), preferred_element_type=jnp.float32
    )
    masked = scores * (1.0 / math.sqrt(HEAD_DIM)) + bias
    unnorm = jnp.exp(masked - jnp.max(masked, axis=-1, keepdims=True))
    probs = unnorm * (1.0 / jnp.sum(unnorm, axis=-1, keepdims=True))
    return jnp.dot(
        probs.astype(jnp.bfloat16), value, preferred_element_type=jnp.float32
    ).astype(jnp.bfloat16)


def mask_bias(query_lag, first_query, queries, keys):
    row = lax.broadcasted_iota(jnp.int32, (queries, keys), 0)
    col = lax.broadcasted_iota(jnp.int32, (queries, keys), 1)
    age = (row + first_query - col).astype(jnp.float32)
    return jnp.where((age >= 0) & (age <= query_lag), 0.0, -1e30)


def weight_of(own, other, pair, kind):
    per_side = own.shape[2] // PAIR
    side = own if pair < per_side else other
    first = (pair % per_side) * PAIR
    return side[kind, :, first : first + PAIR]


def main_kernel(x_ref, own, other, taps_own, taps_other, out_ref, first_ref, pad0, pad1, conv0, conv1, mask_ref, bias_ref):
    frames = x_ref.shape[0]
    width = own.shape[1]
    per_side = own.shape[2] // PAIR
    lag = x_ref[:, width : width + LANES].astype(jnp.float32)
    for step in (1, 2):
        mask_ref[step - 1] = (lag >= step).astype(jnp.float32)
    bias_ref[...] = mask_bias(lag[BACK:, 0:1], BACK, frames - BACK, frames)
    pads, convs, taps = (pad0, pad1), (conv0, conv1), (taps_own, taps_other)
    for pad in pads:
        for kind in range(3):
            pad[kind, 0:8] = jnp.zeros((8, PAIR), jnp.float32)
    for pair in range(2 * per_side + 1):
        if pair < 2 * per_side:
            pad, conv = pads[pair % 2], convs[pair % 2]
            for kind in range(3):
                projected = jnp.dot(
                    x_ref[:, :width], weight_of(own, other, pair, kind), preferred_element_type=jnp.float32
                )
                pad[kind, 8 : 8 + frames] = projected
                first_ref[kind, :, pair * PAIR : (pair + 1) * PAIR] = projected[:BACK]
                convolve(
                    pad.at[kind], conv, taps[pair // per_side], mask_ref, kind,
                    (pair % per_side) * PAIR, frames,
                )
        if pair > 0:
            conv = convs[(pair - 1) % 2]
            for head in range(PAIR // HEAD_DIM):
                columns = slice(head * HEAD_DIM, (head + 1) * HEAD_DIM)
                start = (pair - 1) * PAIR + head * HEAD_DIM
                out_ref[BACK:, start : start + HEAD_DIM] = attend(
                    conv[0, BACK:, columns], conv[1, :, columns], conv[2, :, columns], bias_ref[...]
                )


def halo_kernel(x_ref, lag_ref, own, other, taps_own, taps_other, first_ref, done_ref, out_ref, pad0, pad1, conv0, conv1, mask_ref, bias_ref, result, out_sem):
    del done_ref
    rows = 2 * BACK
    width = own.shape[1]
    per_side = own.shape[2] // PAIR
    halo_lag = x_ref[:, width : width + LANES].astype(jnp.float32)
    lag = lag_ref[...].astype(jnp.float32)
    for step in (1, 2):
        mask_ref[step - 1, :BACK] = (halo_lag >= step).astype(jnp.float32)
        mask_ref[step - 1, BACK:] = (lag >= step).astype(jnp.float32)
    bias_ref[...] = mask_bias(lag[:, 0:1], BACK, BACK, rows)
    pads, convs, taps = (pad0, pad1), (conv0, conv1), (taps_own, taps_other)
    for pad in pads:
        for kind in range(3):
            pad[kind, 0:8] = jnp.zeros((8, PAIR), jnp.float32)
    for pair in range(2 * per_side + 1):
        if pair < 2 * per_side:
            pad, conv = pads[pair % 2], convs[pair % 2]
            for kind in range(3):
                pad[kind, 8 : 8 + BACK] = jnp.dot(
                    x_ref[:, :width], weight_of(own, other, pair, kind), preferred_element_type=jnp.float32
                )
                pad[kind, 8 + BACK : 8 + rows] = first_ref[kind, :, pair * PAIR : (pair + 1) * PAIR]
                convolve(
                    pad.at[kind], conv, taps[pair // per_side], mask_ref, kind,
                    (pair % per_side) * PAIR, rows,
                )
        if pair > 0:
            conv = convs[(pair - 1) % 2]
            for head in range(PAIR // HEAD_DIM):
                columns = slice(head * HEAD_DIM, (head + 1) * HEAD_DIM)
                start = (pair - 1) * PAIR + head * HEAD_DIM
                result[:, start : start + HEAD_DIM] = attend(
                    conv[0, BACK:, columns], conv[1, :, columns], conv[2, :, columns], bias_ref[...]
                )
    copy = pltpu.make_async_copy(result, out_ref.at[pl.ds(0, BACK)], out_sem)
    copy.start()
    copy.wait()


VMEM = pl.BlockSpec(memory_space=pltpu.VMEM)
ANY = pl.BlockSpec(memory_space=pl.ANY)


def scratch(kinds, rows, queries):
    return [
        pltpu.VMEM((kinds, 8 + rows, PAIR), jnp.float32),
        pltpu.VMEM((kinds, 8 + rows, PAIR), jnp.float32),
        pltpu.VMEM((kinds, rows, PAIR), jnp.bfloat16),
        pltpu.VMEM((kinds, rows, PAIR), jnp.bfloat16),
        pltpu.VMEM((2, rows, LANES), jnp.float32),
        pltpu.VMEM((queries, rows), jnp.float32),
    ]


def main_part(rows, own, other, taps):
    frames = rows.shape[0]
    kinds, width, half = own.shape
    inner = 2 * half
    return pl.pallas_call(
        main_kernel,
        out_shape=(
            jax.ShapeDtypeStruct((frames, inner), jnp.bfloat16),
            jax.ShapeDtypeStruct((kinds, BACK, inner), jnp.float32),
        ),
        in_specs=[VMEM, VMEM, VMEM, VMEM, VMEM],
        out_specs=(VMEM, VMEM),
        scratch_shapes=scratch(kinds, frames, frames - BACK),
        compiler_params=pltpu.CompilerParams(vmem_limit_bytes=LIMIT),
        name="main_rows",
    )(rows, own, other, *taps)


def halo_part(halo, lag, own, other, taps, first, attended):
    kinds, width, half = own.shape
    inner = 2 * half
    return pl.pallas_call(
        halo_kernel,
        out_shape=jax.ShapeDtypeStruct(attended.shape, jnp.bfloat16),
        in_specs=[VMEM, VMEM, VMEM, VMEM, VMEM, VMEM, VMEM, ANY],
        out_specs=ANY,
        scratch_shapes=scratch(kinds, 2 * BACK, BACK)
        + [
            pltpu.VMEM((BACK, inner), jnp.bfloat16),
            pltpu.SemaphoreType.DMA,
        ],
        input_output_aliases={7: 0},
        compiler_params=pltpu.CompilerParams(vmem_limit_bytes=LIMIT),
        name="halo_rows",
    )(halo, lag, own, other, *taps, first, attended)


def shards(tokens, w_qkv, conv_taps, w_out, episode_start):
    frames, positions, model_width = tokens.shape
    inner_width = w_qkv.shape[2]
    share = positions // CORES
    core = lax.axis_index("core")
    device_row = lax.axis_index(("y", "z", "x"))
    out_half = model_width // CORES

    taps_other = lax.ppermute(conv_taps, "core", SWAP)
    tokens_f = lax.dynamic_slice_in_dim(tokens, core * share, share, 1).astype(jnp.float32)
    inv_rms = lax.rsqrt(jnp.mean(tokens_f * tokens_f, axis=-1, keepdims=True) + 1e-06)
    normed = (tokens_f * inv_rms).astype(jnp.bfloat16).transpose(1, 0, 2)
    frame_ids = device_row * frames + jnp.arange(frames, dtype=jnp.int32)
    lag = (frame_ids - episode_start).astype(jnp.bfloat16)
    packed = jnp.concatenate(
        [normed, jnp.broadcast_to(lag[None, :, None], (share, frames, LANES))], axis=2
    )
    packed, taps_other, w_sent = lax.optimization_barrier((packed, taps_other, w_qkv))
    w_other = lax.ppermute(w_sent, "core", SWAP)
    w_own = lax.ppermute(w_sent, "core", [(0, 0), (1, 1)])
    with jax.named_scope("gather"):
        rows = lax.all_to_all(packed, ("z", "x"), 0, 0, tiled=True)
    with jax.named_scope("theirs"):
        theirs = lax.dynamic_slice_in_dim(w_out, (1 - core) * out_half, out_half, 1)
    w_out_other = lax.ppermute(theirs, "core", SWAP)
    with jax.named_scope("mine"):
        mine = lax.dynamic_slice_in_dim(w_out, core * out_half, out_half, 1)
    rows = rows.reshape(GROUP * frames, model_width + LANES)
    halo = lax.ppermute(rows[-BACK:], "y", [(y, y + 1) for y in range(PLANES - 1)])

    taps = (conv_taps, taps_other)
    attended, first = main_part(rows, w_own, w_other, taps)
    attended = halo_part(
        halo, rows[:BACK, model_width:], w_own, w_other, taps, first, attended
    )
    with jax.named_scope("back"):
        back = lax.all_to_all(
            attended.reshape(GROUP, frames, CORES * inner_width), ("z", "x"), 0, 0, tiled=True
        )
    back_other = lax.ppermute(back, "core", SWAP)

    def output(part, first, second):
        flat = part.reshape(share * frames, CORES * inner_width)
        return (
            jnp.dot(flat[:, :inner_width], first, preferred_element_type=jnp.float32)
            + jnp.dot(flat[:, inner_width:], second, preferred_element_type=jnp.float32)
        ).astype(jnp.bfloat16).reshape(share, frames, out_half).transpose(1, 0, 2)

    out_mine = output(back, mine, w_out_other)
    out_other = output(back_other, w_out_other, mine)
    result = jnp.zeros((frames, positions, out_half), jnp.bfloat16)
    result = lax.dynamic_update_slice_in_dim(result, out_mine, core * share, 1)
    return lax.dynamic_update_slice_in_dim(result, out_other, (1 - core) * share, 1)


def solution(mesh):
    grid = Mesh(mesh.devices.reshape(PLANES, ROWS, COLS, CORES), ("y", "z", "x", "core"))
    seq = ("y", "z", "x")
    in_specs = (
        P(seq, None, None),
        P(None, None, "core"),
        P(None, None, "core"),
        P("core", None),
        P(seq),
    )
    return jax.shard_map(
        shards, mesh=grid, in_specs=in_specs, out_specs=P(seq, None, "core"), check_vma=False
    )
```

```python
import functools
import math

import jax
import jax.numpy as jnp
from jax import lax
from jax.experimental import pallas as pl
from jax.experimental.pallas import tpu as pltpu
from jax.sharding import Mesh
from jax.sharding import PartitionSpec as P

HEAD_DIM = 128
BACK = 64
PLANES, ROWS, COLS, CORES = 4, 8, 4, 2
GROUP = ROWS * COLS
LANES = 128
PAIR = 256
LIMIT = 38 * 1024 * 1024
HALO_LIMIT = 16 * 1024 * 1024
SWAP = [(0, 1), (1, 0)]


def convolve(pad, conv, taps_ref, masks, kind, first_column, rows):
    for column in range(0, PAIR, LANES):
        columns = slice(column, column + LANES)
        taps = slice(first_column + column, first_column + column + LANES)
        acc = taps_ref[0, kind, taps][None, :] * pad[8 : 8 + rows, columns]
        for lag in (1, 2):
            acc = acc + (
                taps_ref[lag, kind, taps][None, :] * pad[8 - lag : 8 - lag + rows, columns]
            ) * masks[lag - 1]
        conv[kind, :, columns] = acc.astype(jnp.bfloat16)


def attend(query, key, value, bias):
    scores = lax.dot_general(
        query, key, (((1,), (1,)), ((), ())), preferred_element_type=jnp.float32
    )
    masked = scores * (1.0 / math.sqrt(HEAD_DIM)) + bias
    unnorm = jnp.exp(masked - jnp.max(masked, axis=-1, keepdims=True))
    probs = unnorm * (1.0 / jnp.sum(unnorm, axis=-1, keepdims=True))
    return jnp.dot(
        probs.astype(jnp.bfloat16), value, preferred_element_type=jnp.float32
    ).astype(jnp.bfloat16)


def mask_bias(query_lag, first_query, queries, keys):
    row = lax.broadcasted_iota(jnp.int32, (queries, keys), 0)
    col = lax.broadcasted_iota(jnp.int32, (queries, keys), 1)
    age = (row + first_query - col).astype(jnp.float32)
    return jnp.where((age >= 0) & (age <= query_lag), 0.0, -1e30)


def fetch(streamed, buffer, sems):
    copies = []
    for kind in range(streamed.shape[0]):
        copies.append(pltpu.make_async_copy(streamed.at[kind], buffer.at[kind], sems.at[kind]))
        copies[-1].start()
    return copies


def weight_of(resident, buffer, copies, pair, kind):
    per_side = resident.shape[2] // PAIR
    first = (pair % per_side) * PAIR
    if pair < per_side:
        return resident[kind, :, first : first + PAIR]
    if pair == per_side and copies is not None:
        copies[kind].wait()
    return buffer[kind, :, first : first + PAIR]


def main_kernel(x_ref, resident, streamed, taps_first, taps_second, out_ref, first_ref, buffer, pad0, pad1, conv0, conv1, mask_ref, bias_ref, sems):
    frames = x_ref.shape[0]
    width = resident.shape[1]
    per_side = resident.shape[2] // PAIR
    copies = fetch(streamed, buffer, sems)
    lag = x_ref[:, width : width + LANES].astype(jnp.float32)
    for step in (1, 2):
        mask_ref[step - 1] = (lag >= step).astype(jnp.float32)
    bias_ref[...] = mask_bias(lag[BACK:, 0:1], BACK, frames - BACK, frames)
    pads, convs, taps = (pad0, pad1), (conv0, conv1), (taps_first, taps_second)
    for pad in pads:
        for kind in range(3):
            pad[kind, 0:8] = jnp.zeros((8, PAIR), jnp.float32)
    for pair in range(2 * per_side + 1):
        if pair < 2 * per_side:
            pad, conv = pads[pair % 2], convs[pair % 2]
            for kind in range(3):
                projected = jnp.dot(
                    x_ref[:, :width], weight_of(resident, buffer, copies, pair, kind), preferred_element_type=jnp.float32
                )
                pad[kind, 8 : 8 + frames] = projected
                first_ref[kind, :, pair * PAIR : (pair + 1) * PAIR] = projected[:BACK]
                convolve(
                    pad.at[kind], conv, taps[pair // per_side], mask_ref, kind,
                    (pair % per_side) * PAIR, frames,
                )
        if pair > 0:
            conv = convs[(pair - 1) % 2]
            for head in range(PAIR // HEAD_DIM):
                columns = slice(head * HEAD_DIM, (head + 1) * HEAD_DIM)
                start = (pair - 1) * PAIR + head * HEAD_DIM
                out_ref[BACK:, start : start + HEAD_DIM] = attend(
                    conv[0, BACK:, columns], conv[1, :, columns], conv[2, :, columns], bias_ref[...]
                )


def halo_kernel(x_ref, lag_ref, resident, buffer, taps_first, taps_second, first_ref, done_ref, out_ref, pad0, pad1, conv0, conv1, mask_ref, bias_ref, result, out_sem):
    del done_ref
    rows = 2 * BACK
    width = resident.shape[1]
    per_side = resident.shape[2] // PAIR
    halo_lag = x_ref[:, width : width + LANES].astype(jnp.float32)
    lag = lag_ref[...].astype(jnp.float32)
    for step in (1, 2):
        mask_ref[step - 1, :BACK] = (halo_lag >= step).astype(jnp.float32)
        mask_ref[step - 1, BACK:] = (lag >= step).astype(jnp.float32)
    bias_ref[...] = mask_bias(lag[:, 0:1], BACK, BACK, rows)
    pads, convs, taps = (pad0, pad1), (conv0, conv1), (taps_first, taps_second)
    for pad in pads:
        for kind in range(3):
            pad[kind, 0:8] = jnp.zeros((8, PAIR), jnp.float32)
    for pair in range(2 * per_side + 1):
        if pair < 2 * per_side:
            pad, conv = pads[pair % 2], convs[pair % 2]
            for kind in range(3):
                pad[kind, 8 : 8 + BACK] = jnp.dot(
                    x_ref[:, :width], weight_of(resident, buffer, None, pair, kind), preferred_element_type=jnp.float32
                )
                pad[kind, 8 + BACK : 8 + rows] = first_ref[kind, :, pair * PAIR : (pair + 1) * PAIR]
                convolve(
                    pad.at[kind], conv, taps[pair // per_side], mask_ref, kind,
                    (pair % per_side) * PAIR, rows,
                )
        if pair > 0:
            conv = convs[(pair - 1) % 2]
            for head in range(PAIR // HEAD_DIM):
                columns = slice(head * HEAD_DIM, (head + 1) * HEAD_DIM)
                start = (pair - 1) * PAIR + head * HEAD_DIM
                result[:, start : start + HEAD_DIM] = attend(
                    conv[0, BACK:, columns], conv[1, :, columns], conv[2, :, columns], bias_ref[...]
                )
    copy = pltpu.make_async_copy(result, out_ref.at[pl.ds(0, BACK)], out_sem)
    copy.start()
    copy.wait()


VMEM = pl.BlockSpec(memory_space=pltpu.VMEM)
ANY = pl.BlockSpec(memory_space=pl.ANY)


def scratch(kinds, rows, queries):
    return [
        pltpu.VMEM((kinds, 8 + rows, PAIR), jnp.float32),
        pltpu.VMEM((kinds, 8 + rows, PAIR), jnp.float32),
        pltpu.VMEM((kinds, rows, PAIR), jnp.bfloat16),
        pltpu.VMEM((kinds, rows, PAIR), jnp.bfloat16),
        pltpu.VMEM((2, rows, LANES), jnp.float32),
        pltpu.VMEM((queries, rows), jnp.float32),
    ]


def main_part(rows, resident, streamed, taps):
    frames = rows.shape[0]
    kinds, width, half = resident.shape
    inner = 2 * half
    return pl.pallas_call(
        main_kernel,
        out_shape=(
            jax.ShapeDtypeStruct((frames, inner), jnp.bfloat16),
            jax.ShapeDtypeStruct((kinds, BACK, inner), jnp.float32),
            jax.ShapeDtypeStruct(streamed.shape, streamed.dtype),
        ),
        in_specs=[VMEM, VMEM, ANY, VMEM, VMEM],
        out_specs=(VMEM, VMEM, VMEM),
        scratch_shapes=scratch(kinds, frames, frames - BACK)
        + [pltpu.SemaphoreType.DMA((kinds,))],
        compiler_params=pltpu.CompilerParams(vmem_limit_bytes=LIMIT),
        name="main_rows",
    )(rows, resident, streamed, *taps)


def halo_part(halo, lag, resident, streamed, taps, first, attended):
    kinds, width, half = resident.shape
    inner = 2 * half
    return pl.pallas_call(
        halo_kernel,
        out_shape=jax.ShapeDtypeStruct(attended.shape, jnp.bfloat16),
        in_specs=[VMEM] * 7 + [ANY],
        out_specs=ANY,
        scratch_shapes=scratch(kinds, 2 * BACK, BACK)
        + [
            pltpu.VMEM((BACK, inner), jnp.bfloat16),
            pltpu.SemaphoreType.DMA,
        ],
        input_output_aliases={7: 0},
        compiler_params=pltpu.CompilerParams(vmem_limit_bytes=HALO_LIMIT),
        name="halo_rows",
    )(halo, lag, resident, streamed, *taps, first, attended)


def shards(tokens, w_qkv, conv_taps, w_out, episode_start):
    frames, positions, model_width = tokens.shape
    inner_width = w_qkv.shape[2]
    share = positions // CORES
    core = lax.axis_index("core")
    device_row = lax.axis_index(("y", "z", "x"))
    out_half = model_width // CORES

    taps_other = lax.ppermute(conv_taps, "core", SWAP)
    tokens_f = lax.dynamic_slice_in_dim(tokens, core * share, share, 1).astype(jnp.float32)
    inv_rms = lax.rsqrt(jnp.mean(tokens_f * tokens_f, axis=-1, keepdims=True) + 1e-06)
    normed = (tokens_f * inv_rms).astype(jnp.bfloat16).transpose(1, 0, 2)
    frame_ids = device_row * frames + jnp.arange(frames, dtype=jnp.int32)
    lag = (frame_ids - episode_start).astype(jnp.bfloat16)
    packed = jnp.concatenate(
        [normed, jnp.broadcast_to(lag[None, :, None], (share, frames, LANES))], axis=2
    )
    packed, taps_other, w_sent = lax.optimization_barrier((packed, taps_other, w_qkv))
    w_other = lax.ppermute(w_sent, "core", SWAP)
    with jax.named_scope("gather"):
        rows = lax.all_to_all(packed, ("z", "x"), 0, 0, tiled=True)
    with jax.named_scope("theirs"):
        theirs = lax.dynamic_slice_in_dim(w_out, (1 - core) * out_half, out_half, 1)
    w_out_other = lax.ppermute(theirs, "core", SWAP)
    with jax.named_scope("mine"):
        mine = lax.dynamic_slice_in_dim(w_out, core * out_half, out_half, 1)
    rows = rows.reshape(GROUP * frames, model_width + LANES)
    halo = lax.ppermute(rows[-BACK:], "y", [(y, y + 1) for y in range(PLANES - 1)])

    taps = (taps_other, conv_taps)
    attended, first, loaded = main_part(rows, w_other, w_qkv, taps)
    attended = halo_part(
        halo, rows[:BACK, model_width:], w_other, loaded, taps, first, attended
    )
    with jax.named_scope("back"):
        back = lax.all_to_all(
            attended.reshape(GROUP, frames, CORES * inner_width), ("z", "x"), 0, 0, tiled=True
        )
    back_other = lax.ppermute(back, "core", SWAP)

    def output(part, first, second):
        flat = part.reshape(share * frames, CORES * inner_width)
        return (
            jnp.dot(flat[:, :inner_width], first, preferred_element_type=jnp.float32)
            + jnp.dot(flat[:, inner_width:], second, preferred_element_type=jnp.float32)
        ).astype(jnp.bfloat16).reshape(share, frames, out_half).transpose(1, 0, 2)

    out_mine = output(back, w_out_other, mine)
    out_other = output(back_other, mine, w_out_other)
    result = jnp.zeros((frames, positions, out_half), jnp.bfloat16)
    result = lax.dynamic_update_slice_in_dim(result, out_mine, core * share, 1)
    return lax.dynamic_update_slice_in_dim(result, out_other, (1 - core) * share, 1)


def solution(mesh):
    grid = Mesh(mesh.devices.reshape(PLANES, ROWS, COLS, CORES), ("y", "z", "x", "core"))
    seq = ("y", "z", "x")
    in_specs = (
        P(seq, None, None),
        P(None, None, "core"),
        P(None, None, "core"),
        P("core", None),
        P(seq),
    )
    return jax.shard_map(
        shards, mesh=grid, in_specs=in_specs, out_specs=P(seq, None, "core"), check_vma=False
    )
```

```python
import functools
import math

import jax
import jax.numpy as jnp
from jax import lax
from jax.experimental import pallas as pl
from jax.experimental.pallas import tpu as pltpu
from jax.sharding import Mesh
from jax.sharding import PartitionSpec as P

HEAD_DIM = 128
BACK = 64
PLANES, ROWS, COLS, CORES = 4, 8, 4, 2
GROUP = ROWS * COLS
LANES = 128
PAIR = 256
LIMIT = 38 * 1024 * 1024
HALO_LIMIT = 16 * 1024 * 1024
SWAP = [(0, 1), (1, 0)]


def convolve(pad, conv, taps_ref, masks, kind, first_column, rows):
    for column in range(0, PAIR, LANES):
        columns = slice(column, column + LANES)
        taps = slice(first_column + column, first_column + column + LANES)
        acc = taps_ref[0, kind, taps][None, :] * pad[8 : 8 + rows, columns]
        for lag in (1, 2):
            acc = acc + (
                taps_ref[lag, kind, taps][None, :] * pad[8 - lag : 8 - lag + rows, columns]
            ) * masks[lag - 1]
        conv[kind, :, columns] = acc.astype(jnp.bfloat16)


def attend(query, key, value, bias):
    scores = lax.dot_general(
        query, key, (((1,), (1,)), ((), ())), preferred_element_type=jnp.float32
    )
    masked = scores * (1.0 / math.sqrt(HEAD_DIM)) + bias
    unnorm = jnp.exp(masked - jnp.max(masked, axis=-1, keepdims=True))
    probs = unnorm * (1.0 / jnp.sum(unnorm, axis=-1, keepdims=True))
    return jnp.dot(
        probs.astype(jnp.bfloat16), value, preferred_element_type=jnp.float32
    ).astype(jnp.bfloat16)


def mask_bias(query_lag, first_query, queries, keys):
    row = lax.broadcasted_iota(jnp.int32, (queries, keys), 0)
    col = lax.broadcasted_iota(jnp.int32, (queries, keys), 1)
    age = (row + first_query - col).astype(jnp.float32)
    return jnp.where((age >= 0) & (age <= query_lag), 0.0, -1e30)


def fetch(streamed, buffer, sems):
    copies = []
    for kind in range(streamed.shape[0]):
        copies.append(pltpu.make_async_copy(streamed.at[kind], buffer.at[kind], sems.at[kind]))
        copies[-1].start()
    return copies


def weight_of(resident, buffer, copies, pair, kind):
    per_side = resident.shape[2] // PAIR
    first = (pair % per_side) * PAIR
    if pair < per_side:
        return resident[kind, :, first : first + PAIR]
    if pair == per_side and copies is not None:
        copies[kind].wait()
    return buffer[kind, :, first : first + PAIR]


def main_kernel(x_ref, resident, streamed, taps_first, taps_second, out_ref, first_ref, buffer, pad0, pad1, conv0, conv1, mask_ref, bias_ref, sems):
    frames = x_ref.shape[0]
    width = resident.shape[1]
    per_side = resident.shape[2] // PAIR
    copies = fetch(streamed, buffer, sems)
    lag = x_ref[:, width : width + LANES].astype(jnp.float32)
    for step in (1, 2):
        mask_ref[step - 1] = (lag >= step).astype(jnp.float32)
    bias_ref[...] = mask_bias(lag[BACK:, 0:1], BACK, frames - BACK, frames)
    pads, convs, taps = (pad0, pad1), (conv0, conv1), (taps_first, taps_second)
    for pad in pads:
        for kind in range(3):
            pad[kind, 0:8] = jnp.zeros((8, PAIR), jnp.float32)
    def attention(pair):
        conv = convs[pair % 2]
        for head in range(PAIR // HEAD_DIM):
            columns = slice(head * HEAD_DIM, (head + 1) * HEAD_DIM)
            start = pair * PAIR + head * HEAD_DIM
            out_ref[BACK:, start : start + HEAD_DIM] = attend(
                conv[0, BACK:, columns], conv[1, :, columns], conv[2, :, columns], bias_ref[...]
            )

    for pair in range(2 * per_side + 1):
        if pair == per_side:
            attention(pair - 1)
        if pair < 2 * per_side:
            pad, conv = pads[pair % 2], convs[pair % 2]
            for kind in range(3):
                projected = jnp.dot(
                    x_ref[:, :width], weight_of(resident, buffer, copies, pair, kind), preferred_element_type=jnp.float32
                )
                pad[kind, 8 : 8 + frames] = projected
                first_ref[kind, :, pair * PAIR : (pair + 1) * PAIR] = projected[:BACK]
                convolve(
                    pad.at[kind], conv, taps[pair // per_side], mask_ref, kind,
                    (pair % per_side) * PAIR, frames,
                )
        if pair > 0 and pair != per_side:
            attention(pair - 1)


def halo_kernel(x_ref, lag_ref, resident, buffer, taps_first, taps_second, first_ref, done_ref, out_ref, pad0, pad1, conv0, conv1, mask_ref, bias_ref, result, out_sem):
    del done_ref
    rows = 2 * BACK
    width = resident.shape[1]
    per_side = resident.shape[2] // PAIR
    halo_lag = x_ref[:, width : width + LANES].astype(jnp.float32)
    lag = lag_ref[...].astype(jnp.float32)
    for step in (1, 2):
        mask_ref[step - 1, :BACK] = (halo_lag >= step).astype(jnp.float32)
        mask_ref[step - 1, BACK:] = (lag >= step).astype(jnp.float32)
    bias_ref[...] = mask_bias(lag[:, 0:1], BACK, BACK, rows)
    pads, convs, taps = (pad0, pad1), (conv0, conv1), (taps_first, taps_second)
    for pad in pads:
        for kind in range(3):
            pad[kind, 0:8] = jnp.zeros((8, PAIR), jnp.float32)
    for pair in range(2 * per_side + 1):
        if pair < 2 * per_side:
            pad, conv = pads[pair % 2], convs[pair % 2]
            for kind in range(3):
                pad[kind, 8 : 8 + BACK] = jnp.dot(
                    x_ref[:, :width], weight_of(resident, buffer, None, pair, kind), preferred_element_type=jnp.float32
                )
                pad[kind, 8 + BACK : 8 + rows] = first_ref[kind, :, pair * PAIR : (pair + 1) * PAIR]
                convolve(
                    pad.at[kind], conv, taps[pair // per_side], mask_ref, kind,
                    (pair % per_side) * PAIR, rows,
                )
        if pair > 0:
            conv = convs[(pair - 1) % 2]
            for head in range(PAIR // HEAD_DIM):
                columns = slice(head * HEAD_DIM, (head + 1) * HEAD_DIM)
                start = (pair - 1) * PAIR + head * HEAD_DIM
                result[:, start : start + HEAD_DIM] = attend(
                    conv[0, BACK:, columns], conv[1, :, columns], conv[2, :, columns], bias_ref[...]
                )
    copy = pltpu.make_async_copy(result, out_ref.at[pl.ds(0, BACK)], out_sem)
    copy.start()
    copy.wait()


VMEM = pl.BlockSpec(memory_space=pltpu.VMEM)
ANY = pl.BlockSpec(memory_space=pl.ANY)


def scratch(kinds, rows, queries):
    return [
        pltpu.VMEM((kinds, 8 + rows, PAIR), jnp.float32),
        pltpu.VMEM((kinds, 8 + rows, PAIR), jnp.float32),
        pltpu.VMEM((kinds, rows, PAIR), jnp.bfloat16),
        pltpu.VMEM((kinds, rows, PAIR), jnp.bfloat16),
        pltpu.VMEM((2, rows, LANES), jnp.float32),
        pltpu.VMEM((queries, rows), jnp.float32),
    ]


def main_part(rows, resident, streamed, taps):
    frames = rows.shape[0]
    kinds, width, half = resident.shape
    inner = 2 * half
    return pl.pallas_call(
        main_kernel,
        out_shape=(
            jax.ShapeDtypeStruct((frames, inner), jnp.bfloat16),
            jax.ShapeDtypeStruct((kinds, BACK, inner), jnp.float32),
            jax.ShapeDtypeStruct(streamed.shape, streamed.dtype),
        ),
        in_specs=[VMEM, VMEM, ANY, VMEM, VMEM],
        out_specs=(VMEM, VMEM, VMEM),
        scratch_shapes=scratch(kinds, frames, frames - BACK)
        + [pltpu.SemaphoreType.DMA((kinds,))],
        compiler_params=pltpu.CompilerParams(vmem_limit_bytes=LIMIT),
        name="main_rows",
    )(rows, resident, streamed, *taps)


def halo_part(halo, lag, resident, streamed, taps, first, attended):
    kinds, width, half = resident.shape
    inner = 2 * half
    return pl.pallas_call(
        halo_kernel,
        out_shape=jax.ShapeDtypeStruct(attended.shape, jnp.bfloat16),
        in_specs=[VMEM] * 7 + [ANY],
        out_specs=ANY,
        scratch_shapes=scratch(kinds, 2 * BACK, BACK)
        + [
            pltpu.VMEM((BACK, inner), jnp.bfloat16),
            pltpu.SemaphoreType.DMA,
        ],
        input_output_aliases={7: 0},
        compiler_params=pltpu.CompilerParams(vmem_limit_bytes=HALO_LIMIT),
        name="halo_rows",
    )(halo, lag, resident, streamed, *taps, first, attended)


def shards(tokens, w_qkv, conv_taps, w_out, episode_start):
    frames, positions, model_width = tokens.shape
    inner_width = w_qkv.shape[2]
    share = positions // CORES
    core = lax.axis_index("core")
    device_row = lax.axis_index(("y", "z", "x"))
    out_half = model_width // CORES

    taps_other = lax.ppermute(conv_taps, "core", SWAP)
    tokens_f = lax.dynamic_slice_in_dim(tokens, core * share, share, 1).astype(jnp.float32)
    inv_rms = lax.rsqrt(jnp.mean(tokens_f * tokens_f, axis=-1, keepdims=True) + 1e-06)
    normed = (tokens_f * inv_rms).astype(jnp.bfloat16).transpose(1, 0, 2)
    frame_ids = device_row * frames + jnp.arange(frames, dtype=jnp.int32)
    lag = (frame_ids - episode_start).astype(jnp.bfloat16)
    packed = jnp.concatenate(
        [normed, jnp.broadcast_to(lag[None, :, None], (share, frames, LANES))], axis=2
    )
    packed, taps_other, w_sent = lax.optimization_barrier((packed, taps_other, w_qkv))
    w_other = lax.ppermute(w_sent, "core", SWAP)
    with jax.named_scope("gather"):
        rows = lax.all_to_all(packed, ("z", "x"), 0, 0, tiled=True)
    with jax.named_scope("theirs"):
        theirs = lax.dynamic_slice_in_dim(w_out, (1 - core) * out_half, out_half, 1)
    w_out_other = lax.ppermute(theirs, "core", SWAP)
    with jax.named_scope("mine"):
        mine = lax.dynamic_slice_in_dim(w_out, core * out_half, out_half, 1)
    rows = rows.reshape(GROUP * frames, model_width + LANES)
    halo = lax.ppermute(rows[-BACK:], "y", [(y, y + 1) for y in range(PLANES - 1)])

    taps = (taps_other, conv_taps)
    attended, first, loaded = main_part(rows, w_other, w_qkv, taps)
    attended = halo_part(
        halo, rows[:BACK, model_width:], w_other, loaded, taps, first, attended
    )
    with jax.named_scope("back"):
        back = lax.all_to_all(
            attended.reshape(GROUP, frames, CORES * inner_width), ("z", "x"), 0, 0, tiled=True
        )
    back_other = lax.ppermute(back, "core", SWAP)

    def output(part, first, second):
        flat = part.reshape(share * frames, CORES * inner_width)
        return (
            jnp.dot(flat[:, :inner_width], first, preferred_element_type=jnp.float32)
            + jnp.dot(flat[:, inner_width:], second, preferred_element_type=jnp.float32)
        ).astype(jnp.bfloat16).reshape(share, frames, out_half).transpose(1, 0, 2)

    out_mine = output(back, w_out_other, mine)
    out_other = output(back_other, mine, w_out_other)
    result = jnp.zeros((frames, positions, out_half), jnp.bfloat16)
    result = lax.dynamic_update_slice_in_dim(result, out_mine, core * share, 1)
    return lax.dynamic_update_slice_in_dim(result, out_other, (1 - core) * share, 1)


def solution(mesh):
    grid = Mesh(mesh.devices.reshape(PLANES, ROWS, COLS, CORES), ("y", "z", "x", "core"))
    seq = ("y", "z", "x")
    in_specs = (
        P(seq, None, None),
        P(None, None, "core"),
        P(None, None, "core"),
        P("core", None),
        P(seq),
    )
    return jax.shard_map(
        shards, mesh=grid, in_specs=in_specs, out_specs=P(seq, None, "core"), check_vma=False
    )
```
